256 devices in a mesh: gz: 64 (over x, y, z_lo, core), gy: 4 (over z_hi).
Axes of the slice: x: 4, y: 4, z: 8 (z_hi: 4, z_lo: 2; z = z_hi * 2 + z_lo), core: 2. Of those that a mesh axis runs over, the one named last changes fastest.
Arguments:
- coarse_six: float32 [512, 1024, 512], P('gz', 'gy'), may hold values from 0.1 to 10
Outputs:
- detail_seven: float32 [512, 1024, 512], P('gz', 'gy')
- coarse_seven: float32 [512, 1024, 512], P('gz', 'gy')
The draws below stay inside these ranges and needn't reach their ends.
All inputs are finite; a program needn't handle non-finite values.
Results may differ from the reference program's by a relative error of at most 0.00002.
Values sent between devices are 32-bit elements; how exact they have to be, the bound alone decides.
A program may use at most 128 MiB of HBM per device.

```python
import math
import jax
import jax.numpy as jnp

NX = 512
TAP_DILATION = 32
NZ = 512
NY = 1024


def steps_of(own_key, extent, cuts, smallest, top_value):
    def one(position, parts):
        heights = jax.random.uniform(jax.random.fold_in(jax.random.fold_in(own_key, 6), position), (parts,), jnp.float32, smallest / len(cuts), top_value / len(cuts))
        return jnp.repeat(jnp.exp(heights), extent[position] // parts).reshape((-1,) + (1,) * (len(extent) - position - 1))

    loudness = one(*cuts[0])
    for cut in cuts[1:]:
        loudness = loudness * one(*cut)
    return loudness


def setup_inputs(seed: int = 0) -> dict:
    key_of = jax.random.split(jax.random.key(seed), 2)
    coarse_six = jnp.clip(jnp.exp(math.log(10.0) - 4.6051702 * jax.random.uniform(key_of[0], (NZ, NY, NX), jnp.float32) ** steps_of(key_of[0], (NZ, NY, NX), ((0, 64), (1, 4)), -0.2, 0.2)), 0.1, 10.0)
    return {"coarse_six": coarse_six}


kernel_weights = (0.0625, 0.25, 0.375, 0.25, 0.0625)


def smooth_axis(density_field, axis_ordinal):
    weighted_total = jnp.zeros_like(density_field)
    for cell_position in range(5):
        weighted_total = weighted_total + kernel_weights[cell_position] * jnp.roll(density_field, -(cell_position - 2) * TAP_DILATION, axis=axis_ordinal)
    return weighted_total


def reference(coarse_six):
    along_z = smooth_axis(coarse_six, 0)
    along_y = smooth_axis(along_z, 1)
    coarse_seven = smooth_axis(along_y, 2)
    return coarse_six - coarse_seven, coarse_seven
```

```python
import functools

import jax
import jax.numpy as jnp
from jax import lax
from jax.experimental import pallas as pl
from jax.experimental.pallas import tpu as pltpu
from jax.sharding import PartitionSpec as P

MESH = pl.DeviceIdType.MESH
F32 = jnp.float32

PLANES, ROWS, COLS = 8, 256, 512
RING = 16
PIECE = ROWS // RING
DIL = 32
HALO = 2 * DIL
EARLY = 2
SCALE = 1.0 / 4096.0
HOPS = tuple((a, b) for a in range(4) for b in range(4) if a or b)


def place():
    g, h = lax.axis_index("gz"), lax.axis_index("gy")
    return g // 16, (g // 4) % 4, g % 4, h


def device(dx, dy):
    x, y, r, h = place()
    return (((x + dx) % 4) * 16 + ((y + dy) % 4) * 4 + r, h)


def ring_index(dx, dy):
    x, y, _, _ = place()
    return ((x + dx) % 4) * 4 + (y + dy) % 4


def gy_device(dh):
    g, h = lax.axis_index("gz"), lax.axis_index("gy")
    return (g, (h + dh) % 4)


def smooth_x(src, dst, j):
    lane = lax.broadcasted_iota(jnp.int32, (8, 128), 1)
    low, high = lane < 96, lane >= 32

    def row_tile(t):
        rows = pl.ds(pl.multiple_of(t * 8, 8), 8)
        v = [src[j, rows, 128 * k : 128 * k + 128] for k in range(4)]
        for _ in range(2):
            r = [pltpu.roll(a, 96, 1) for a in v]
            v = [v[k] + jnp.where(low, r[k], r[(k + 1) % 4]) for k in range(4)]
            r = [pltpu.roll(a, 32, 1) for a in v]
            v = [v[k] + jnp.where(high, r[k], r[(k + 3) % 4]) for k in range(4)]
        for k in range(4):
            dst[j, rows, 128 * k : 128 * k + 128] = v[k]

    @pl.loop(0, ROWS // 32)
    def _(t):
        for u in range(4):
            row_tile(t * 4 + u)


def smooth_y(src, before, after, j, emit):
    @pl.loop(0, DIL // 8)
    def _(t):
        for k in range(4):
            cols = slice(128 * k, 128 * k + 128)

            def at(ref, start):
                return ref[j, pl.ds(pl.multiple_of(start + t * 8, 8), 8), cols]

            v = [at(before, 0), at(before, DIL)]
            v += [at(src, DIL * i) for i in range(ROWS // DIL)]
            v += [at(after, 0), at(after, DIL)]
            for _ in range(4):
                v = [v[i] + v[i + 1] for i in range(len(v) - 1)]
            for i in range(ROWS // DIL):
                emit(pl.ds(pl.multiple_of(DIL * i + t * 8, 8), 8), cols, v[i])


def smooth_z(src, dst, j):
    for t in range(PIECE // 8):
        for k in range(4):
            rows, cols = slice(8 * t, 8 * t + 8), slice(128 * k, 128 * k + 128)
            v = [src[j, q, rows, cols] for q in range(RING)]
            for _ in range(4):
                v = [v[q] + v[(q + 1) % RING] for q in range(RING)]
            for q in range(RING):
                dst[j, q, rows, cols] = v[(q - 2) % RING] * SCALE


def kernel(x_ref, detail_ref, coarse_ref, xin, xs, ys, gathered, smoothed, back, before, after, detail,
           load_sem, f_send, f_recv, b_send, b_recv, h_send, h_recv, o_sem):
    me = ring_index(0, 0)

    def load(j):
        return pltpu.make_async_copy(x_ref.at[j], xin.at[j], load_sem.at[j])

    def forth(j, src, k):
        dx, dy = HOPS[k]
        rows = pl.ds(pl.multiple_of(ring_index(dx, dy) * PIECE, PIECE), PIECE)
        return pltpu.make_async_remote_copy(
            src.at[j, rows], gathered.at[j, me], f_send.at[j, k], f_recv.at[j, k],
            device_id=device(dx, dy), device_id_type=MESH)

    def home(j, k):
        dx, dy = HOPS[k]
        rows = pl.ds(pl.multiple_of(me * PIECE, PIECE), PIECE)
        return pltpu.make_async_remote_copy(
            smoothed.at[j, ring_index(dx, dy)], back.at[j, rows], b_send.at[j, k], b_recv.at[j, k],
            device_id=device(dx, dy), device_id_type=MESH)

    def halo(j, src, side):
        if side == 0:
            return pltpu.make_async_remote_copy(
                src.at[j, pl.ds(ROWS - HALO, HALO)], before.at[j], h_send.at[j, 0], h_recv.at[j, 0],
                device_id=gy_device(1), device_id_type=MESH)
        return pltpu.make_async_remote_copy(
            src.at[j, pl.ds(0, HALO)], after.at[j], h_send.at[j, 1], h_recv.at[j, 1],
            device_id=gy_device(3), device_id_type=MESH)

    def store(j, which):
        src, dst = ((detail, detail_ref), (back, coarse_ref))[which]
        return pltpu.make_async_copy(src.at[j], dst.at[j], o_sem.at[j, which])

    mine = pl.ds(pl.multiple_of(me * PIECE, PIECE), PIECE)

    def send_forth(j, src):
        for k in range(len(HOPS)):
            forth(j, src, k).start()
        gathered[j, me] = src[j, mine]

    def step_z(j):
        for k in range(len(HOPS)):
            forth(j, xs, k).wait_recv()
        smooth_z(gathered, smoothed, j)
        for k in range(len(HOPS)):
            home(j, k).start()
        back[j, mine] = smoothed[j, me]

    def step_y(j):
        for side in range(2):
            halo(j, xs, side).wait_recv()

        def emit(rows, cols, value):
            ys[j, rows, cols] = value

        smooth_y(xs, before, after, j, emit)
        send_forth(j, ys)

    def finish(j):
        @pl.loop(0, ROWS // 32)
        def _(t):
            rows = pl.ds(pl.multiple_of(t * 32, 32), 32)
            detail[j, rows] = xin[j, rows] - back[j, rows]

        store(j, 0).start()
        store(j, 1).start()

    for j in range(PLANES):
        load(j).start()
    barrier = pltpu.get_barrier_semaphore()
    for dx, dy in HOPS:
        pl.semaphore_signal(barrier, inc=1, device_id=device(dx, dy), device_id_type=MESH)
    for dh in (1, 3):
        pl.semaphore_signal(barrier, inc=1, device_id=gy_device(dh), device_id_type=MESH)
    load(0).wait()
    smooth_x(xin, xs, 0)
    pl.semaphore_wait(barrier, len(HOPS) + 2)
    send_forth(0, xs)

    @pl.loop(1, EARLY)
    def _(j):
        load(j).wait()
        smooth_x(xin, xs, j)
        send_forth(j, xs)

    @pl.loop(EARLY, PLANES)
    def _(j):
        load(j).wait()
        smooth_x(xin, xs, j)
        for side in range(2):
            halo(j, xs, side).start()

    @pl.loop(0, PLANES)
    def _(i):
        @pl.when(i < PLANES - EARLY)
        def _():
            step_y(i + EARLY)

        step_z(i)

        @pl.when((i >= 3) & (i < 3 + EARLY))
        def _():
            j = i - 3
            for k in range(len(HOPS)):
                home(j, k).wait_recv()
            for side in range(2):
                halo(j, back, side).start()

    @pl.loop(0, EARLY)
    def _(j):
        for side in range(2):
            halo(j, back, side).wait()

        def emit(rows, cols, value):
            ys[j, rows, cols] = value

        smooth_y(back, before, after, j, emit)

        @pl.loop(0, ROWS // 32)
        def _(t):
            rows = pl.ds(pl.multiple_of(t * 32, 32), 32)
            back[j, rows] = ys[j, rows]

        finish(j)

    @pl.loop(EARLY, PLANES)
    def _(j):
        for k in range(len(HOPS)):
            home(j, k).wait_recv()
        finish(j)

    @pl.loop(EARLY, PLANES)
    def _(j):
        for side in range(2):
            halo(j, xs, side).wait_send()

    @pl.loop(0, PLANES)
    def _(j):
        for k in range(len(HOPS)):
            forth(j, xs, k).wait_send()
            home(j, k).wait_send()
        store(j, 0).wait()
        store(j, 1).wait()


def shards(coarse_six):
    block = jax.ShapeDtypeStruct((PLANES, ROWS, COLS), F32)
    full = pltpu.VMEM((PLANES, ROWS, COLS), F32)
    pieces = pltpu.VMEM((PLANES, RING, PIECE, COLS), F32)
    edge = pltpu.VMEM((PLANES, HALO, COLS), F32)
    dma = pltpu.SemaphoreType.DMA
    n = len(HOPS)
    return pl.pallas_call(
        kernel,
        out_shape=(block, block),
        in_specs=[pl.BlockSpec(memory_space=pl.ANY)],
        out_specs=(pl.BlockSpec(memory_space=pl.ANY),) * 2,
        scratch_shapes=[full, full, full, pieces, pieces, full, edge, edge, full,
                        dma((PLANES,)), dma((PLANES, n)), dma((PLANES, n)), dma((PLANES, n)), dma((PLANES, n)),
                        dma((PLANES, 2)), dma((PLANES, 2)), dma((PLANES, 2))],
        compiler_params=pltpu.CompilerParams(collective_id=0, has_side_effects=True, vmem_limit_bytes=44 << 20),
        name="starlet",
    )(coarse_six)


def solution(mesh):
    return jax.shard_map(
        shards,
        mesh=mesh,
        in_specs=(P("gz", "gy", None),),
        out_specs=(P("gz", "gy", None), P("gz", "gy", None)),
        check_vma=False,
    )
```

```python
import functools

import jax
import jax.numpy as jnp
from jax import lax
from jax.experimental import pallas as pl
from jax.experimental.pallas import tpu as pltpu
from jax.sharding import PartitionSpec as P

MESH = pl.DeviceIdType.MESH
F32 = jnp.float32

PLANES, ROWS, COLS = 8, 256, 512
RING = 4
PIECE = ROWS // RING
TILES = PIECE // 8
SENT = 3 * TILES + TILES - 2
DIL = 32
HALO = 2 * DIL
EARLY = 4
LAGZ, LAG1, LAG2 = 1, 4, 6
SCALE = 1.0 / 4096.0
HOPS = (1, 3, 2)
GREET = ((0, 1), (0, 2), (0, 3), (1, 0), (3, 0))


def place():
    g, h = lax.axis_index("gz"), lax.axis_index("gy")
    return g // 16, (g // 4) % 4, g % 4, h


def device(dx, dy):
    x, y, r, h = place()
    return (((x + dx) % 4) * 16 + ((y + dy) % 4) * 4 + r, h)


def ring_index(dy):
    return (place()[1] + dy) % 4


def gy_device(dh):
    g, h = lax.axis_index("gz"), lax.axis_index("gy")
    return (g, (h + dh) % 4)


def tile(start):
    return pl.ds(pl.multiple_of(start, 8), 8)


def smooth_x(src, j, emit):
    lane = lax.broadcasted_iota(jnp.int32, (8, 128), 1)
    left, low, high = lane < 64, lane < 96, lane >= 32

    @pl.loop(0, ROWS // 32)
    def _(t):
        for u in range(4):
            v = [src[j, tile(t * 32 + 8 * u), 128 * k : 128 * k + 128] for k in range(4)]
            up = [pltpu.roll(a, 96, 1) for a in v]
            half = [pltpu.roll(a, 64, 1) for a in v]
            down = [pltpu.roll(a, 32, 1) for a in v]
            for k in range(4):
                after, before = (k + 1) % 4, (k + 3) % 4
                near = jnp.where(low, up[k], up[after]) + jnp.where(high, down[k], down[before])
                far = half[k] + jnp.where(left, half[before], half[after])
                emit(t, 8 * u, k, 6.0 * v[k] + (4.0 * near + far))


def smooth_y(src, before, after, j, emit):
    @pl.loop(0, DIL // 8)
    def _(t):
        for k in range(4):
            cols = slice(128 * k, 128 * k + 128)

            def at(ref, start):
                return ref[j, tile(start + t * 8), cols]

            v = [at(before, 0), at(before, DIL)]
            v += [at(src, DIL * i) for i in range(ROWS // DIL)]
            v += [at(after, 0), at(after, DIL)]
            for _ in range(4):
                v = [v[i] + v[i + 1] for i in range(len(v) - 1)]
            for i in range(ROWS // DIL):
                emit(i, t * 8, k, v[i])


def pack_last(column, dst, j):
    low = lax.broadcasted_iota(jnp.int32, (8, 128), 1) < 96
    for p in range(RING):
        v = [column[PIECE * p + 8 * t : PIECE * p + 8 * t + 8, :] for t in range(TILES)]
        for t in range(TILES - 2):
            moved = pltpu.roll(v[TILES - 2 + t // 3], 96 - 32 * (t % 3), 1)
            dst[j, p, 8 * (3 * TILES + t) : 8 * (3 * TILES + t) + 8, :] = jnp.where(low, v[t], moved)


def unpack(src, j, emit):
    lane = lax.broadcasted_iota(jnp.int32, (8, 128), 1)
    low, one, two = lane < 96, lane < 32, lane < 64
    odd = (lane // 32) % 2 == 1

    @pl.loop(0, RING)
    def _(p):
        last = [src[j, p, 8 * (3 * TILES + t) : 8 * (3 * TILES + t) + 8, :] for t in range(TILES - 2)]
        for t in (0, 3):
            r = [pltpu.roll(last[t + i], 32 * i + 32, 1) for i in range(3)]
            last.append(jnp.where(one, r[0], jnp.where(two, r[1], r[2])))
        for t in range(TILES):
            v = [src[j, p, 8 * (k * TILES + t) : 8 * (k * TILES + t) + 8, :] for k in range(3)]
            total = (v[0] + v[1]) + (v[2] + jnp.where(low, last[t], 0.0))
            total = jnp.where(odd, -total, total)
            total = total + pltpu.roll(total, 64, 1)
            total = total + pltpu.roll(total, 32, 1)
            v.append(jnp.where(low, last[t], total))
            for k in range(4):
                emit(p, 8 * t, k, v[k])


def smooth_z(src, dst, j):
    @pl.loop(0, SENT // 3)
    def _(t):
        for u in range(3):
            rows = tile(t * 24 + 8 * u)
            v = [src[j, q, rows, :] for q in range(RING + 4)]
            for _ in range(4):
                v = [v[q] + v[q + 1] for q in range(len(v) - 1)]
            for q in range(RING):
                dst[j, q, rows, :] = v[q] * SCALE


def kernel(x_ref, detail, coarse, xin, xs, ys, column, gathered, smoothed, back, early, before, after,
           load_sem, f_send, f_recv, b_send, b_recv, h_send, h_recv, x_send, x_recv):
    me = ring_index(0)
    hops = range(len(HOPS))

    def load(j):
        return pltpu.make_async_copy(x_ref.at[j], xin.at[j], load_sem.at[j])

    def forth(j, k):
        dy = HOPS[k]
        return pltpu.make_async_remote_copy(
            ys.at[j, ring_index(dy)], gathered.at[j, me + 2], f_send.at[j, k], f_recv.at[j, k],
            device_id=device(0, dy), device_id_type=MESH)

    def home(j, k):
        dy = HOPS[k]
        return pltpu.make_async_remote_copy(
            smoothed.at[j, ring_index(dy)], back.at[j, me], b_send.at[j, k], b_recv.at[j, k],
            device_id=device(0, dy), device_id_type=MESH)

    def halo(j, src, side):
        if side == 0:
            return pltpu.make_async_remote_copy(
                src.at[j, pl.ds(ROWS - HALO, HALO)], before.at[j], h_send.at[j, 0], h_recv.at[j, 0],
                device_id=gy_device(1), device_id_type=MESH)
        return pltpu.make_async_remote_copy(
            src.at[j, pl.ds(0, HALO)], after.at[j], h_send.at[j, 1], h_recv.at[j, 1],
            device_id=gy_device(3), device_id_type=MESH)

    def emit_packed(j, block, row, k, value):
        if k < 3:
            ys[j, block // 2, tile(PIECE * k + 32 * (block % 2) + row), :] = value
        else:
            column[tile(32 * block + row), :] = value

    def send_forth(j):
        pack_last(column, ys, j)
        for k in hops:
            forth(j, k).start()
        gathered[j, me + 2] = ys[j, me]

    def across(j, side):
        src, dst, dx = ((4, 0, 1), (2, 6, 3))[side]
        return pltpu.make_async_remote_copy(
            gathered.at[j, pl.ds(src, 2)], gathered.at[j, pl.ds(dst, 2)], x_send.at[j, side], x_recv.at[j, side],
            device_id=device(dx, 0), device_id_type=MESH)

    def step_x(j):
        for k in hops:
            forth(j, k).wait_recv()
        for side in range(2):
            across(j, side).start()

    def step_z(j):
        for side in range(2):
            across(j, side).wait_recv()
        smooth_z(gathered, smoothed, j)
        for k in hops:
            home(j, k).start()
        back[j, me] = smoothed[j, me]

    def step_y(j):
        for side in range(2):
            halo(j, xs, side).wait_recv()
        smooth_y(xs, before, after, j, lambda block, row, k, value: emit_packed(j, block, row, k, value))
        send_forth(j)

    def early_halo(j):
        for k in hops:
            home(j, k).wait_recv()

        def emit(p, row, k, value):
            early[j, tile(PIECE * p + row), 128 * k : 128 * k + 128] = value

        unpack(back, j, emit)
        for side in range(2):
            halo(j, early, side).start()

    def emit_out(j, start, k, value):
        rows, cols = tile(start), slice(128 * k, 128 * k + 128)
        coarse[j, rows, cols] = value
        detail[j, rows, cols] = xin[j, rows, cols] - value

    def early_finish(j):
        for side in range(2):
            halo(j, early, side).wait_recv()
        smooth_y(early, before, after, j, lambda block, row, k, value: emit_out(j, 32 * block + row, k, value))

    def late_finish(j):
        for k in hops:
            home(j, k).wait_recv()
        unpack(back, j, lambda p, row, k, value: emit_out(j, PIECE * p + row, k, value))

    def early_start(j):
        smooth_x(xin, j, lambda block, row, k, value: emit_packed(j, block, row, k, value))

    def late_start(j):
        def emit(block, row, k, value):
            xs[j, tile(32 * block + row), 128 * k : 128 * k + 128] = value

        smooth_x(xin, j, emit)
        for side in range(2):
            halo(j, xs, side).start()

    for j in range(PLANES):
        load(j).start()
    barrier = pltpu.get_barrier_semaphore()
    for dx, dy in GREET:
        pl.semaphore_signal(barrier, inc=1, device_id=device(dx, dy), device_id_type=MESH)
    for dh in (1, 3):
        pl.semaphore_signal(barrier, inc=1, device_id=gy_device(dh), device_id_type=MESH)
    load(0).wait()
    early_start(0)
    pl.semaphore_wait(barrier, len(GREET) + 2)
    send_forth(0)

    @pl.loop(1, EARLY)
    def _(j):
        load(j).wait()
        early_start(j)
        send_forth(j)

    @pl.loop(EARLY, PLANES)
    def _(j):
        load(j).wait()
        late_start(j)

    @pl.loop(0, PLANES + LAG2)
    def _(i):
        @pl.when(i < PLANES - EARLY)
        def _():
            step_y(i + EARLY)

        @pl.when(i < PLANES)
        def _():
            step_x(i)

        @pl.when((i >= LAGZ) & (i < LAGZ + PLANES))
        def _():
            step_z(i - LAGZ)

        @pl.when((i >= LAG1) & (i < LAG1 + EARLY))
        def _():
            early_halo(i - LAG1)

        @pl.when((i >= LAG2) & (i < LAG2 + EARLY))
        def _():
            early_finish(i - LAG2)

        @pl.when(i >= LAG2 + EARLY)
        def _():
            late_finish(i - LAG2)

    @pl.loop(0, PLANES)
    def _(j):
        for side in range(2):
            halo(j, xs, side).wait_send()
            across(j, side).wait_send()
        for k in hops:
            forth(j, k).wait_send()
            home(j, k).wait_send()


def shards(coarse_six):
    full = pltpu.VMEM((PLANES, ROWS, COLS), F32)

    def packed(n):
        return pltpu.VMEM((PLANES, n, 8 * SENT, 128), F32)

    edge = pltpu.VMEM((PLANES, HALO, COLS), F32)
    dma = pltpu.SemaphoreType.DMA
    n = len(HOPS)
    return pl.pallas_call(
        kernel,
        out_shape=(full, full),
        in_specs=[pl.BlockSpec(memory_space=pl.ANY)],
        out_specs=(pl.BlockSpec(memory_space=pltpu.VMEM),) * 2,
        scratch_shapes=[full, full, packed(RING), pltpu.VMEM((ROWS, 128), F32), packed(RING + 4), packed(RING), packed(RING),
                        pltpu.VMEM((EARLY, ROWS, COLS), F32), edge, edge,
                        dma((PLANES,)), dma((PLANES, n)), dma((PLANES, n)), dma((PLANES, n)), dma((PLANES, n)),
                        dma((PLANES, 2)), dma((PLANES, 2)), dma((PLANES, 2)), dma((PLANES, 2))],
        compiler_params=pltpu.CompilerParams(collective_id=0, has_side_effects=True, vmem_limit_bytes=50 << 20),
        name="starlet",
    )(coarse_six)


def solution(mesh):
    return jax.shard_map(
        shards,
        mesh=mesh,
        in_specs=(P("gz", "gy", None),),
        out_specs=(P("gz", "gy", None), P("gz", "gy", None)),
        check_vma=False,
    )
```

```python
import functools

import jax
import jax.numpy as jnp
from jax import lax
from jax.experimental import pallas as pl
from jax.experimental.pallas import tpu as pltpu
from jax.sharding import PartitionSpec as P

MESH = pl.DeviceIdType.MESH
F32 = jnp.float32

PLANES, ROWS, COLS = 8, 256, 512
RING = 4
PIECE = ROWS // RING
TILES = PIECE // 8
SENT = 3 * TILES + TILES - 2
DIL = 32
HALO = 2 * DIL
EARLY = 4
LAGZ, LAG1, LAG2 = 1, 4, 6
SCALE = 1.0 / 4096.0
HOPS = (1, 3, 2)


def place():
    g, h = lax.axis_index("gz"), lax.axis_index("gy")
    return g // 16, (g // 4) % 4, g % 4, h


def device(dx, dy):
    x, y, r, h = place()
    return (((x + dx) % 4) * 16 + ((y + dy) % 4) * 4 + r, h)


def ring_index(dy):
    return (place()[1] + dy) % 4


def gy_device(dh):
    g, h = lax.axis_index("gz"), lax.axis_index("gy")
    return (g, (h + dh) % 4)


def tile(start):
    return pl.ds(pl.multiple_of(start, 8), 8)


def smooth_x(src, j, emit, first=0, count=ROWS // 32):
    lane = lax.broadcasted_iota(jnp.int32, (8, 128), 1)
    left, low, high = lane < 64, lane < 96, lane >= 32

    @pl.loop(first, first + count)
    def _(t):
        for u in range(4):
            v = [src[j, tile(t * 32 + 8 * u), 128 * k : 128 * k + 128] for k in range(4)]
            up = [pltpu.roll(a, 96, 1) for a in v]
            half = [pltpu.roll(a, 64, 1) for a in v]
            down = [pltpu.roll(a, 32, 1) for a in v]
            for k in range(4):
                after, before = (k + 1) % 4, (k + 3) % 4
                near = jnp.where(low, up[k], up[after]) + jnp.where(high, down[k], down[before])
                far = half[k] + jnp.where(left, half[before], half[after])
                emit(t, 8 * u, k, 6.0 * v[k] + (4.0 * near + far))


def smooth_y(src, before, after, j, emit):
    @pl.loop(0, DIL // 8)
    def _(t):
        for k in range(4):
            cols = slice(128 * k, 128 * k + 128)

            def at(ref, start):
                return ref[j, tile(start + t * 8), cols]

            v = [at(before, 0), at(before, DIL)]
            v += [at(src, DIL * i) for i in range(ROWS // DIL)]
            v += [at(after, 0), at(after, DIL)]
            for _ in range(4):
                v = [v[i] + v[i + 1] for i in range(len(v) - 1)]
            for i in range(ROWS // DIL):
                emit(i, t * 8, k, v[i])


def pack_last(column, dst, j, p):
    low = lax.broadcasted_iota(jnp.int32, (8, 128), 1) < 96
    v = [column[tile(PIECE * p + 8 * t), :] for t in range(TILES)]
    for t in range(TILES - 2):
        moved = pltpu.roll(v[TILES - 2 + t // 3], 96 - 32 * (t % 3), 1)
        dst[j, p, 8 * (3 * TILES + t) : 8 * (3 * TILES + t) + 8, :] = jnp.where(low, v[t], moved)


def unpack(src, j, p, emit):
    lane = lax.broadcasted_iota(jnp.int32, (8, 128), 1)
    low, one, two = lane < 96, lane < 32, lane < 64
    odd = (lane // 32) % 2 == 1

    last = [src[j, p, 8 * (3 * TILES + t) : 8 * (3 * TILES + t) + 8, :] for t in range(TILES - 2)]
    for t in (0, 3):
        r = [pltpu.roll(last[t + i], 32 * i + 32, 1) for i in range(3)]
        last.append(jnp.where(one, r[0], jnp.where(two, r[1], r[2])))
    for t in range(TILES):
        v = [src[j, p, 8 * (k * TILES + t) : 8 * (k * TILES + t) + 8, :] for k in range(3)]
        total = (v[0] + v[1]) + (v[2] + jnp.where(low, last[t], 0.0))
        total = jnp.where(odd, -total, total)
        total = total + pltpu.roll(total, 64, 1)
        total = total + pltpu.roll(total, 32, 1)
        v.append(jnp.where(low, last[t], total))
        for k in range(4):
            emit(p, 8 * t, k, v[k])


def smooth_z(src, dst, j):
    @pl.loop(0, SENT // 3)
    def _(t):
        for u in range(3):
            rows = tile(t * 24 + 8 * u)
            v = [src[j, q, rows, :] for q in range(RING + 4)]
            for _ in range(4):
                v = [v[q] + v[q + 1] for q in range(len(v) - 1)]
            for q in range(RING):
                dst[j, q, rows, :] = v[q] * SCALE


def kernel(x_ref, detail, coarse, xin, xs, ys, column, gathered, smoothed, back, early, before, after,
           ring_sem, near_sem, load_sem, first_sem, f_send, f_recv, b_send, b_recv, h_send, h_recv, x_send, x_recv):
    me = ring_index(0)
    hops = range(len(HOPS))

    def load(j):
        return pltpu.make_async_copy(x_ref.at[j], xin.at[j], load_sem.at[j])

    def load_first(dy):
        rows = pl.ds(pl.multiple_of(PIECE * ring_index(dy), PIECE), PIECE)
        return pltpu.make_async_copy(x_ref.at[0, rows], xin.at[0, rows], first_sem.at[dy])

    def forth(j, k):
        dy = HOPS[k]
        return pltpu.make_async_remote_copy(
            ys.at[j, ring_index(dy)], gathered.at[j, me + 2], f_send.at[j, k], f_recv.at[j, k],
            device_id=device(0, dy), device_id_type=MESH)

    def home(j, k):
        dy = HOPS[k]
        return pltpu.make_async_remote_copy(
            smoothed.at[j, ring_index(dy)], back.at[j, me], b_send.at[j, k], b_recv.at[j, k],
            device_id=device(0, dy), device_id_type=MESH)

    def halo(j, src, side):
        if side == 0:
            return pltpu.make_async_remote_copy(
                src.at[j, pl.ds(ROWS - HALO, HALO)], before.at[j], h_send.at[j, 0], h_recv.at[j, 0],
                device_id=gy_device(1), device_id_type=MESH)
        return pltpu.make_async_remote_copy(
            src.at[j, pl.ds(0, HALO)], after.at[j], h_send.at[j, 1], h_recv.at[j, 1],
            device_id=gy_device(3), device_id_type=MESH)

    def emit_packed(j, block, row, k, value):
        if k < 3:
            ys[j, block // 2, tile(PIECE * k + 32 * (block % 2) + row), :] = value
        else:
            column[tile(32 * block + row), :] = value

    def send_forth(j):
        for k in hops:
            pack_last(column, ys, j, ring_index(HOPS[k]))
            forth(j, k).start()
        pack_last(column, ys, j, me)
        gathered[j, me + 2] = ys[j, me]

    def across(j, side):
        src, dst, dx = ((4, 0, 1), (2, 6, 3))[side]
        return pltpu.make_async_remote_copy(
            gathered.at[j, pl.ds(src, 2)], gathered.at[j, pl.ds(dst, 2)], x_send.at[j, side], x_recv.at[j, side],
            device_id=device(dx, 0), device_id_type=MESH)

    def step_x(j):
        for k in hops:
            forth(j, k).wait_recv()
        for side in range(2):
            across(j, side).start()

    def step_z(j):
        for side in range(2):
            across(j, side).wait_recv()
        smooth_z(gathered, smoothed, j)
        for k in hops:
            home(j, k).start()
        back[j, me] = smoothed[j, me]

    def step_y(j):
        for side in range(2):
            halo(j, xs, side).wait_recv()
        smooth_y(xs, before, after, j, lambda block, row, k, value: emit_packed(j, block, row, k, value))
        send_forth(j)

    def arrive(j, emit):
        unpack(back, j, me, emit)
        for k in hops:
            home(j, k).wait_recv()
            unpack(back, j, ring_index(-HOPS[k]), emit)

    def early_halo(j):
        def emit(p, row, k, value):
            early[j, tile(PIECE * p + row), 128 * k : 128 * k + 128] = value

        arrive(j, emit)
        for side in range(2):
            halo(j, early, side).start()

    def emit_out(j, start, k, value):
        rows, cols = tile(start), slice(128 * k, 128 * k + 128)
        coarse[j, rows, cols] = value
        detail[j, rows, cols] = xin[j, rows, cols] - value

    def early_finish(j):
        for side in range(2):
            halo(j, early, side).wait_recv()
        sent(j)
        smooth_y(early, before, after, j, lambda block, row, k, value: emit_out(j, 32 * block + row, k, value))

    def sent(j):
        for side in range(2):
            halo(j, xs, side).wait_send()
            across(j, side).wait_send()
        for k in hops:
            forth(j, k).wait_send()

        @pl.when(j > 0)
        def _():
            for k in hops:
                home(j - 1, k).wait_send()

    def late_finish(j):
        sent(j)
        arrive(j, lambda p, row, k, value: emit_out(j, PIECE * p + row, k, value))

    def early_start(j):
        smooth_x(xin, j, lambda block, row, k, value: emit_packed(j, block, row, k, value))

    def late_start(j):
        def emit(block, row, k, value):
            xs[j, tile(32 * block + row), 128 * k : 128 * k + 128] = value

        smooth_x(xin, j, emit)

    for dy in HOPS + (0,):
        load_first(dy).start()
    y = place()[1]
    barrier = pltpu.get_barrier_semaphore()
    for dy in HOPS:
        @pl.when((y + dy) % 4 != 0)
        def _():
            pl.semaphore_signal(barrier, inc=1, device_id=device(0, dy), device_id_type=MESH)

    for j in range(1, PLANES):
        load(j).start()

    def first_piece(dy):
        load_first(dy).wait()
        p = ring_index(dy)
        smooth_x(xin, 0, lambda block, row, k, value: emit_packed(0, block, row, k, value), 2 * p, 2)
        pack_last(column, ys, 0, p)

    first_piece(HOPS[0])

    @pl.when(y != 0)
    def _():
        pl.semaphore_wait(barrier, 3)
        pl.semaphore_signal(ring_sem, inc=1, device_id=device(0, 4 - y), device_id_type=MESH)

    @pl.when(y == 0)
    def _():
        pl.semaphore_wait(ring_sem, 3)
        for there in (device(1, 0), device(3, 0), gy_device(1), gy_device(3)):
            pl.semaphore_signal(barrier, inc=1, device_id=there, device_id_type=MESH)

    forth(0, 0).start()
    for k in hops[1:]:
        first_piece(HOPS[k])
        forth(0, k).start()
    first_piece(0)
    gathered[0, me + 2] = ys[0, me]

    @pl.loop(1, EARLY)
    def _(j):
        load(j).wait()
        early_start(j)
        send_forth(j)

    @pl.loop(EARLY, PLANES)
    def _(j):
        load(j).wait()
        late_start(j)

    @pl.when(y == 0)
    def _():
        pl.semaphore_wait(barrier, 4)
        for dy in HOPS:
            pl.semaphore_signal(near_sem, inc=1, device_id=device(0, dy), device_id_type=MESH)

    @pl.when(y != 0)
    def _():
        pl.semaphore_wait(near_sem, 1)

    @pl.loop(EARLY, PLANES)
    def _(j):
        for side in range(2):
            halo(j, xs, side).start()

    @pl.loop(0, PLANES + LAG2)
    def _(i):
        @pl.when(i < PLANES - EARLY)
        def _():
            step_y(i + EARLY)

        @pl.when(i < PLANES)
        def _():
            step_x(i)

        @pl.when((i >= LAGZ) & (i < LAGZ + PLANES))
        def _():
            step_z(i - LAGZ)

        @pl.when((i >= LAG1) & (i < LAG1 + EARLY))
        def _():
            early_halo(i - LAG1)

        @pl.when((i >= LAG2) & (i < LAG2 + EARLY))
        def _():
            early_finish(i - LAG2)

        @pl.when(i >= LAG2 + EARLY)
        def _():
            late_finish(i - LAG2)

    for k in hops:
        home(PLANES - 1, k).wait_send()


def shards(coarse_six):
    full = pltpu.VMEM((PLANES, ROWS, COLS), F32)

    def packed(n):
        return pltpu.VMEM((PLANES, n, 8 * SENT, 128), F32)

    edge = pltpu.VMEM((PLANES, HALO, COLS), F32)
    dma = pltpu.SemaphoreType.DMA
    n = len(HOPS)
    return pl.pallas_call(
        kernel,
        out_shape=(full, full),
        in_specs=[pl.BlockSpec(memory_space=pl.ANY)],
        out_specs=(pl.BlockSpec(memory_space=pltpu.VMEM),) * 2,
        scratch_shapes=[full, full, packed(RING), pltpu.VMEM((ROWS, 128), F32), packed(RING + 4), packed(RING), packed(RING),
                        pltpu.VMEM((EARLY, ROWS, COLS), F32), edge, edge,
                        pltpu.SemaphoreType.REGULAR, pltpu.SemaphoreType.REGULAR, dma((PLANES,)), dma((RING,)), dma((PLANES, n)), dma((PLANES, n)), dma((PLANES, n)), dma((PLANES, n)),
                        dma((PLANES, 2)), dma((PLANES, 2)), dma((PLANES, 2)), dma((PLANES, 2))],
        compiler_params=pltpu.CompilerParams(collective_id=0, has_side_effects=True, vmem_limit_bytes=50 << 20),
        name="starlet",
    )(coarse_six)


def solution(mesh):
    return jax.shard_map(
        shards,
        mesh=mesh,
        in_specs=(P("gz", "gy", None),),
        out_specs=(P("gz", "gy", None), P("gz", "gy", None)),
        check_vma=False,
    )
```

```python
import functools

import jax
import jax.numpy as jnp
from jax import lax
from jax.experimental import pallas as pl
from jax.experimental.pallas import tpu as pltpu
from jax.sharding import PartitionSpec as P

MESH = pl.DeviceIdType.MESH
F32 = jnp.float32

PLANES, ROWS, COLS = 8, 256, 512
RING = 4
PIECE = ROWS // RING
TILES = PIECE // 8
SENT = 3 * TILES + TILES - 2
DIL = 32
HALO = 2 * DIL
EARLY = 5
LAGY, LAGZ, LAG1, LAG2 = 1, 1, 4, 6
SCALE = 1.0 / 4096.0
HOPS = (1, 3, 2)


def place():
    g, h = lax.axis_index("gz"), lax.axis_index("gy")
    return g // 16, (g // 4) % 4, g % 4, h


def device(dx, dy):
    x, y, r, h = place()
    return (((x + dx) % 4) * 16 + ((y + dy) % 4) * 4 + r, h)


def ring_index(dy):
    return (place()[1] + dy) % 4


def gy_device(dh):
    g, h = lax.axis_index("gz"), lax.axis_index("gy")
    return (g, (h + dh) % 4)


def tile(start):
    return pl.ds(pl.multiple_of(start, 8), 8)


def smooth_x(src, j, emit, first=0, count=ROWS // 32):
    lane = lax.broadcasted_iota(jnp.int32, (8, 128), 1)
    left, low, high = lane < 64, lane < 96, lane >= 32

    @pl.loop(first, first + count)
    def _(t):
        for u in range(4):
            v = [src[j, tile(t * 32 + 8 * u), 128 * k : 128 * k + 128] for k in range(4)]
            up = [pltpu.roll(a, 96, 1) for a in v]
            half = [pltpu.roll(a, 64, 1) for a in v]
            down = [pltpu.roll(a, 32, 1) for a in v]
            for k in range(4):
                after, before = (k + 1) % 4, (k + 3) % 4
                near = jnp.where(low, up[k], up[after]) + jnp.where(high, down[k], down[before])
                far = half[k] + jnp.where(left, half[before], half[after])
                emit(t, 8 * u, k, 6.0 * v[k] + (4.0 * near + far))


def smooth_y(src, before, after, j, emit):
    @pl.loop(0, DIL // 8)
    def _(t):
        for k in range(4):
            cols = slice(128 * k, 128 * k + 128)

            def at(ref, start):
                return ref[j, tile(start + t * 8), cols]

            v = [at(before, 0), at(before, DIL)]
            v += [at(src, DIL * i) for i in range(ROWS // DIL)]
            v += [at(after, 0), at(after, DIL)]
            for _ in range(4):
                v = [v[i] + v[i + 1] for i in range(len(v) - 1)]
            for i in range(ROWS // DIL):
                emit(i, t * 8, k, v[i])


def pack_last(column, dst, j, p):
    low = lax.broadcasted_iota(jnp.int32, (8, 128), 1) < 96
    v = [column[tile(PIECE * p + 8 * t), :] for t in range(TILES)]
    for t in range(TILES - 2):
        moved = pltpu.roll(v[TILES - 2 + t // 3], 96 - 32 * (t % 3), 1)
        dst[j, p, 8 * (3 * TILES + t) : 8 * (3 * TILES + t) + 8, :] = jnp.where(low, v[t], moved)


def unpack(src, j, p, emit):
    lane = lax.broadcasted_iota(jnp.int32, (8, 128), 1)
    low, one, two = lane < 96, lane < 32, lane < 64
    odd = (lane // 32) % 2 == 1

    last = [src[j, p, 8 * (3 * TILES + t) : 8 * (3 * TILES + t) + 8, :] for t in range(TILES - 2)]
    for t in (0, 3):
        r = [pltpu.roll(last[t + i], 32 * i + 32, 1) for i in range(3)]
        last.append(jnp.where(one, r[0], jnp.where(two, r[1], r[2])))
    for t in range(TILES):
        v = [src[j, p, 8 * (k * TILES + t) : 8 * (k * TILES + t) + 8, :] for k in range(3)]
        total = (v[0] + v[1]) + (v[2] + jnp.where(low, last[t], 0.0))
        total = jnp.where(odd, -total, total)
        total = total + pltpu.roll(total, 64, 1)
        total = total + pltpu.roll(total, 32, 1)
        v.append(jnp.where(low, last[t], total))
        for k in range(4):
            emit(p, 8 * t, k, v[k])


def smooth_z(src, dst, j):
    @pl.loop(0, SENT // 3)
    def _(t):
        for u in range(3):
            rows = tile(t * 24 + 8 * u)
            v = [src[j, q, rows, :] for q in range(RING + 4)]
            for _ in range(4):
                v = [v[q] + v[q + 1] for q in range(len(v) - 1)]
            for q in range(RING):
                dst[j, q, rows, :] = v[q] * SCALE


def kernel(x_ref, detail, coarse, xin, xs, ys, column, gathered, smoothed, back, early, before, after,
           ring_sem, near_sem, load_sem, first_sem, f_send, f_recv, b_send, b_recv, h_send, h_recv, x_send, x_recv):
    me = ring_index(0)
    hops = range(len(HOPS))

    def load(j):
        return pltpu.make_async_copy(x_ref.at[j], xin.at[j], load_sem.at[j])

    def load_first(dy):
        rows = pl.ds(pl.multiple_of(PIECE * ring_index(dy), PIECE), PIECE)
        return pltpu.make_async_copy(x_ref.at[0, rows], xin.at[0, rows], first_sem.at[dy])

    def forth(j, k):
        dy = HOPS[k]
        return pltpu.make_async_remote_copy(
            ys.at[j, ring_index(dy)], gathered.at[j, me + 2], f_send.at[j, k], f_recv.at[j, k],
            device_id=device(0, dy), device_id_type=MESH)

    def home(j, k):
        dy = HOPS[k]
        return pltpu.make_async_remote_copy(
            smoothed.at[j, ring_index(dy)], back.at[j, me], b_send.at[j, k], b_recv.at[j, k],
            device_id=device(0, dy), device_id_type=MESH)

    def halo(j, src, side):
        if side == 0:
            return pltpu.make_async_remote_copy(
                src.at[j, pl.ds(ROWS - HALO, HALO)], before.at[j], h_send.at[j, 0], h_recv.at[j, 0],
                device_id=gy_device(1), device_id_type=MESH)
        return pltpu.make_async_remote_copy(
            src.at[j, pl.ds(0, HALO)], after.at[j], h_send.at[j, 1], h_recv.at[j, 1],
            device_id=gy_device(3), device_id_type=MESH)

    def emit_packed(j, block, row, k, value):
        if k < 3:
            ys[j, block // 2, tile(PIECE * k + 32 * (block % 2) + row), :] = value
        else:
            column[tile(32 * block + row), :] = value

    def send_forth(j):
        for k in hops:
            pack_last(column, ys, j, ring_index(HOPS[k]))
            forth(j, k).start()
        pack_last(column, ys, j, me)
        gathered[j, me + 2] = ys[j, me]

    def across(j, side):
        src, dst, dx = ((4, 0, 1), (2, 6, 3))[side]
        return pltpu.make_async_remote_copy(
            gathered.at[j, pl.ds(src, 2)], gathered.at[j, pl.ds(dst, 2)], x_send.at[j, side], x_recv.at[j, side],
            device_id=device(dx, 0), device_id_type=MESH)

    def step_x(j):
        for k in hops:
            forth(j, k).wait_recv()
        for side in range(2):
            across(j, side).start()

    def step_z(j):
        for side in range(2):
            across(j, side).wait_recv()
        smooth_z(gathered, smoothed, j)
        for k in hops:
            home(j, k).start()
        back[j, me] = smoothed[j, me]

    def step_y(j):
        for side in range(2):
            halo(j, xs, side).wait_recv()
        smooth_y(xs, before, after, j, lambda block, row, k, value: emit_packed(j, block, row, k, value))
        send_forth(j)

    def arrive(j, emit):
        unpack(back, j, me, emit)
        for k in hops:
            home(j, k).wait_recv()
            unpack(back, j, ring_index(-HOPS[k]), emit)

    def early_halo(j):
        def emit(p, row, k, value):
            early[j, tile(PIECE * p + row), 128 * k : 128 * k + 128] = value

        arrive(j, emit)
        for side in range(2):
            halo(j, early, side).start()

    def emit_out(j, start, k, value):
        rows, cols = tile(start), slice(128 * k, 128 * k + 128)
        coarse[j, rows, cols] = value
        detail[j, rows, cols] = xin[j, rows, cols] - value

    def early_finish(j):
        for side in range(2):
            halo(j, early, side).wait_recv()
        sent(j)
        smooth_y(early, before, after, j, lambda block, row, k, value: emit_out(j, 32 * block + row, k, value))

    def sent(j):
        for side in range(2):
            halo(j, xs, side).wait_send()
            across(j, side).wait_send()
        for k in hops:
            forth(j, k).wait_send()

        @pl.when(j > 0)
        def _():
            for k in hops:
                home(j - 1, k).wait_send()

    def late_finish(j):
        sent(j)
        arrive(j, lambda p, row, k, value: emit_out(j, PIECE * p + row, k, value))

    def early_start(j):
        smooth_x(xin, j, lambda block, row, k, value: emit_packed(j, block, row, k, value))

    def late_start(j):
        def emit(block, row, k, value):
            xs[j, tile(32 * block + row), 128 * k : 128 * k + 128] = value

        smooth_x(xin, j, emit)

    for dy in HOPS + (0,):
        load_first(dy).start()
    y = place()[1]
    barrier = pltpu.get_barrier_semaphore()
    for dy in HOPS:
        @pl.when((y + dy) % 4 != 0)
        def _():
            pl.semaphore_signal(barrier, inc=1, device_id=device(0, dy), device_id_type=MESH)

    for j in range(1, PLANES):
        load(j).start()

    def first_piece(dy):
        load_first(dy).wait()
        p = ring_index(dy)
        smooth_x(xin, 0, lambda block, row, k, value: emit_packed(0, block, row, k, value), 2 * p, 2)
        pack_last(column, ys, 0, p)

    first_piece(HOPS[0])

    @pl.when(y != 0)
    def _():
        pl.semaphore_wait(barrier, 3)
        pl.semaphore_signal(ring_sem, inc=1, device_id=device(0, 4 - y), device_id_type=MESH)

    @pl.when(y == 0)
    def _():
        pl.semaphore_wait(ring_sem, 3)
        for there in (device(1, 0), device(3, 0), gy_device(1), gy_device(3)):
            pl.semaphore_signal(barrier, inc=1, device_id=there, device_id_type=MESH)

    forth(0, 0).start()
    for k in hops[1:]:
        first_piece(HOPS[k])
        forth(0, k).start()
    first_piece(0)
    gathered[0, me + 2] = ys[0, me]

    @pl.loop(1, EARLY)
    def _(j):
        load(j).wait()
        early_start(j)
        send_forth(j)

    @pl.loop(EARLY, PLANES)
    def _(j):
        load(j).wait()
        late_start(j)

    @pl.when(y == 0)
    def _():
        pl.semaphore_wait(barrier, 4)
        for dy in HOPS:
            pl.semaphore_signal(near_sem, inc=1, device_id=device(0, dy), device_id_type=MESH)

    @pl.when(y != 0)
    def _():
        pl.semaphore_wait(near_sem, 1)

    @pl.loop(EARLY, PLANES)
    def _(j):
        for side in range(2):
            halo(j, xs, side).start()

    @pl.loop(0, PLANES + LAG2)
    def _(i):
        @pl.when(i < PLANES)
        def _():
            step_x(i)

        @pl.when((i >= LAGZ) & (i < LAGZ + PLANES))
        def _():
            step_z(i - LAGZ)

        @pl.when((i >= LAGY) & (i < LAGY + PLANES - EARLY))
        def _():
            step_y(i + EARLY - LAGY)

        @pl.when((i >= LAG1) & (i < LAG1 + EARLY))
        def _():
            early_halo(i - LAG1)

        @pl.when((i >= LAG2) & (i < LAG2 + EARLY))
        def _():
            early_finish(i - LAG2)

        @pl.when(i >= LAG2 + EARLY)
        def _():
            late_finish(i - LAG2)

    for k in hops:
        home(PLANES - 1, k).wait_send()


def shards(coarse_six):
    full = pltpu.VMEM((PLANES, ROWS, COLS), F32)

    def packed(n):
        return pltpu.VMEM((PLANES, n, 8 * SENT, 128), F32)

    edge = pltpu.VMEM((PLANES, HALO, COLS), F32)
    dma = pltpu.SemaphoreType.DMA
    n = len(HOPS)
    return pl.pallas_call(
        kernel,
        out_shape=(full, full),
        in_specs=[pl.BlockSpec(memory_space=pl.ANY)],
        out_specs=(pl.BlockSpec(memory_space=pltpu.VMEM),) * 2,
        scratch_shapes=[full, full, packed(RING), pltpu.VMEM((ROWS, 128), F32), packed(RING + 4), packed(RING), packed(RING),
                        pltpu.VMEM((EARLY, ROWS, COLS), F32), edge, edge,
                        pltpu.SemaphoreType.REGULAR, pltpu.SemaphoreType.REGULAR, dma((PLANES,)), dma((RING,)), dma((PLANES, n)), dma((PLANES, n)), dma((PLANES, n)), dma((PLANES, n)),
                        dma((PLANES, 2)), dma((PLANES, 2)), dma((PLANES, 2)), dma((PLANES, 2))],
        compiler_params=pltpu.CompilerParams(collective_id=0, has_side_effects=True, vmem_limit_bytes=50 << 20),
        name="starlet",
    )(coarse_six)


def solution(mesh):
    return jax.shard_map(
        shards,
        mesh=mesh,
        in_specs=(P("gz", "gy", None),),
        out_specs=(P("gz", "gy", None), P("gz", "gy", None)),
        check_vma=False,
    )
```

```python
import functools

import jax
import jax.numpy as jnp
from jax import lax
from jax.experimental import pallas as pl
from jax.experimental.pallas import tpu as pltpu
from jax.sharding import PartitionSpec as P

MESH = pl.DeviceIdType.MESH
F32 = jnp.float32

PLANES, ROWS, COLS = 8, 256, 512
RING = 4
PIECE = ROWS // RING
TILES = PIECE // 8
SENT = 3 * TILES + TILES - 2
DIL = 32
HALO = 2 * DIL
EARLY = 5
LAGY, LAGZ, LAG1, LAG2 = 1, 1, 4, 6
SCALE = 1.0 / 4096.0
HOPS = (1, 3, 2)


def place():
    g, h = lax.axis_index("gz"), lax.axis_index("gy")
    return g // 16, (g // 4) % 4, g % 4, h


def device(dx, dy):
    x, y, r, h = place()
    return (((x + dx) % 4) * 16 + ((y + dy) % 4) * 4 + r, h)


def ring_index(dy):
    return (place()[1] + dy) % 4


def gy_device(dh):
    g, h = lax.axis_index("gz"), lax.axis_index("gy")
    return (g, (h + dh) % 4)


def tile(start):
    return pl.ds(pl.multiple_of(start, 8), 8)


def smooth_x(src, j, emit, first=0, count=ROWS // 32):
    lane = lax.broadcasted_iota(jnp.int32, (8, 128), 1)
    left, low, high = lane < 64, lane < 96, lane >= 32

    @pl.loop(first, first + count)
    def _(t):
        for u in range(4):
            v = [src[j, tile(t * 32 + 8 * u), 128 * k : 128 * k + 128] for k in range(4)]
            up = [pltpu.roll(a, 96, 1) for a in v]
            half = [pltpu.roll(a, 64, 1) for a in v]
            down = [pltpu.roll(a, 32, 1) for a in v]
            for k in range(4):
                after, before = (k + 1) % 4, (k + 3) % 4
                near = jnp.where(low, up[k], up[after]) + jnp.where(high, down[k], down[before])
                far = half[k] + jnp.where(left, half[before], half[after])
                emit(t, 8 * u, k, 6.0 * v[k] + (4.0 * near + far))


def smooth_y(src, before, after, j, emit):
    @pl.loop(0, DIL // 8)
    def _(t):
        for k in range(4):
            cols = slice(128 * k, 128 * k + 128)

            def at(ref, start):
                return ref[j, tile(start + t * 8), cols]

            v = [at(before, 0), at(before, DIL)]
            v += [at(src, DIL * i) for i in range(ROWS // DIL)]
            v += [at(after, 0), at(after, DIL)]
            for _ in range(4):
                v = [v[i] + v[i + 1] for i in range(len(v) - 1)]
            for i in range(ROWS // DIL):
                emit(i, t * 8, k, v[i])


def pack_last(column, dst, j, p):
    low = lax.broadcasted_iota(jnp.int32, (8, 128), 1) < 96
    v = [column[tile(PIECE * p + 8 * t), :] for t in range(TILES)]
    for t in range(TILES - 2):
        moved = pltpu.roll(v[TILES - 2 + t // 3], 96 - 32 * (t % 3), 1)
        dst[j, p, 8 * (3 * TILES + t) : 8 * (3 * TILES + t) + 8, :] = jnp.where(low, v[t], moved)


def unpack(src, j, p, emit):
    lane = lax.broadcasted_iota(jnp.int32, (8, 128), 1)
    low, one, two = lane < 96, lane < 32, lane < 64
    odd = (lane // 32) % 2 == 1

    last = [src[j, p, 8 * (3 * TILES + t) : 8 * (3 * TILES + t) + 8, :] for t in range(TILES - 2)]
    for t in (0, 3):
        r = [pltpu.roll(last[t + i], 32 * i + 32, 1) for i in range(3)]
        last.append(jnp.where(one, r[0], jnp.where(two, r[1], r[2])))
    for t in range(TILES):
        v = [src[j, p, 8 * (k * TILES + t) : 8 * (k * TILES + t) + 8, :] for k in range(3)]
        total = (v[0] + v[1]) + (v[2] + jnp.where(low, last[t], 0.0))
        total = jnp.where(odd, -total, total)
        total = total + pltpu.roll(total, 64, 1)
        total = total + pltpu.roll(total, 32, 1)
        v.append(jnp.where(low, last[t], total))
        for k in range(4):
            emit(p, 8 * t, k, v[k])


def smooth_z(src, dst, j):
    @pl.loop(0, SENT // 3)
    def _(t):
        for u in range(3):
            rows = tile(t * 24 + 8 * u)
            v = [src[j, q, rows, :] for q in range(RING + 4)]
            for _ in range(4):
                v = [v[q] + v[q + 1] for q in range(len(v) - 1)]
            for q in range(RING):
                dst[j, q, rows, :] = v[q] * SCALE


def kernel(x_ref, detail, coarse, xin, xs, ys, column, gathered, smoothed, back, early, before, after,
           ring_sem, near_sem, load_sem, first_sem, f_send, f_recv, b_send, b_recv, h_send, h_recv, x_send, x_recv):
    me = ring_index(0)
    hops = range(len(HOPS))

    def load(j):
        return pltpu.make_async_copy(x_ref.at[j], xin.at[j], load_sem.at[j])

    def load_first(dy):
        rows = pl.ds(pl.multiple_of(PIECE * ring_index(dy), PIECE), PIECE)
        return pltpu.make_async_copy(x_ref.at[0, rows], xin.at[0, rows], first_sem.at[dy])

    def forth(j, k):
        dy = HOPS[k]
        return pltpu.make_async_remote_copy(
            ys.at[j, ring_index(dy)], gathered.at[j, me + 2], f_send.at[j, k], f_recv.at[j, k],
            device_id=device(0, dy), device_id_type=MESH)

    def home(j, k):
        dy = HOPS[k]
        return pltpu.make_async_remote_copy(
            smoothed.at[j, ring_index(dy)], back.at[j, me], b_send.at[j, k], b_recv.at[j, k],
            device_id=device(0, dy), device_id_type=MESH)

    def halo(j, src, side):
        if side == 0:
            return pltpu.make_async_remote_copy(
                src.at[j, pl.ds(ROWS - HALO, HALO)], before.at[j], h_send.at[j, 0], h_recv.at[j, 0],
                device_id=gy_device(1), device_id_type=MESH)
        return pltpu.make_async_remote_copy(
            src.at[j, pl.ds(0, HALO)], after.at[j], h_send.at[j, 1], h_recv.at[j, 1],
            device_id=gy_device(3), device_id_type=MESH)

    def emit_packed(j, block, row, k, value):
        if k < 3:
            ys[j, block // 2, tile(PIECE * k + 32 * (block % 2) + row), :] = value
        else:
            column[tile(32 * block + row), :] = value

    def send_forth(j):
        for k in hops:
            pack_last(column, ys, j, ring_index(HOPS[k]))
            forth(j, k).start()
        pack_last(column, ys, j, me)
        gathered[j, me + 2] = ys[j, me]

    def across(j, side):
        src, dst, dx = ((4, 0, 1), (2, 6, 3))[side]
        return pltpu.make_async_remote_copy(
            gathered.at[j, pl.ds(src, 2)], gathered.at[j, pl.ds(dst, 2)], x_send.at[j, side], x_recv.at[j, side],
            device_id=device(dx, 0), device_id_type=MESH)

    def step_x(j):
        for k in hops:
            forth(j, k).wait_recv()
        for side in range(2):
            across(j, side).start()

    def step_z(j):
        for side in range(2):
            across(j, side).wait_recv()
        smooth_z(gathered, smoothed, j)
        for k in hops:
            home(j, k).start()
        back[j, me] = smoothed[j, me]

    def step_y(j):
        for side in range(2):
            halo(j, xs, side).wait_recv()
        smooth_y(xs, before, after, j, lambda block, row, k, value: emit_packed(j, block, row, k, value))
        send_forth(j)

    def arrive(j, emit):
        unpack(back, j, me, emit)
        for k in hops:
            home(j, k).wait_recv()
            unpack(back, j, ring_index(-HOPS[k]), emit)

    def early_halo(j):
        def emit(p, row, k, value):
            early[j, tile(PIECE * p + row), 128 * k : 128 * k + 128] = value

        arrive(j, emit)
        for side in range(2):
            halo(j, early, side).start()

    def emit_out(j, start, k, value):
        rows, cols = tile(start), slice(128 * k, 128 * k + 128)
        coarse[j, rows, cols] = value
        detail[j, rows, cols] = xin[j, rows, cols] - value

    def early_finish(j):
        for side in range(2):
            halo(j, early, side).wait_recv()
        sent(j)
        smooth_y(early, before, after, j, lambda block, row, k, value: emit_out(j, 32 * block + row, k, value))

    def sent(j):
        for side in range(2):
            halo(j, xs, side).wait_send()
            across(j, side).wait_send()
        for k in hops:
            forth(j, k).wait_send()

        @pl.when(j > 0)
        def _():
            for k in hops:
                home(j - 1, k).wait_send()

    def late_finish(j):
        sent(j)
        arrive(j, lambda p, row, k, value: emit_out(j, PIECE * p + row, k, value))

    def early_start(j):
        smooth_x(xin, j, lambda block, row, k, value: emit_packed(j, block, row, k, value))

    def late_start(j):
        def emit(block, row, k, value):
            xs[j, tile(32 * block + row), 128 * k : 128 * k + 128] = value

        smooth_x(xin, j, emit)

    for dy in HOPS + (0,):
        load_first(dy).start()
    y = place()[1]
    barrier = pltpu.get_barrier_semaphore()
    for dy in HOPS:
        @pl.when((y + dy) % 4 != 0)
        def _():
            pl.semaphore_signal(barrier, inc=1, device_id=device(0, dy), device_id_type=MESH)

    for j in range(1, PLANES):
        load(j).start()

    def first_piece(dy):
        load_first(dy).wait()
        p = ring_index(dy)
        smooth_x(xin, 0, lambda block, row, k, value: emit_packed(0, block, row, k, value), 2 * p, 2)
        pack_last(column, ys, 0, p)

    first_piece(HOPS[0])

    @pl.when(y != 0)
    def _():
        pl.semaphore_wait(barrier, 3)
        pl.semaphore_signal(ring_sem, inc=1, device_id=device(0, 4 - y), device_id_type=MESH)

    @pl.when(y == 0)
    def _():
        pl.semaphore_wait(ring_sem, 3)
        for there in (device(1, 0), device(3, 0), gy_device(1), gy_device(3)):
            pl.semaphore_signal(barrier, inc=1, device_id=there, device_id_type=MESH)

    forth(0, 0).start()
    for k in hops[1:]:
        first_piece(HOPS[k])
        forth(0, k).start()
    first_piece(0)
    gathered[0, me + 2] = ys[0, me]

    @pl.loop(1, EARLY)
    def _(j):
        load(j).wait()
        early_start(j)
        send_forth(j)

    @pl.loop(EARLY, PLANES)
    def _(j):
        load(j).wait()
        late_start(j)

    @pl.when(y == 0)
    def _():
        pl.semaphore_wait(barrier, 4)
        for dy in HOPS:
            pl.semaphore_signal(near_sem, inc=1, device_id=device(0, dy), device_id_type=MESH)

    @pl.when(y != 0)
    def _():
        pl.semaphore_wait(near_sem, 1)

    @pl.loop(EARLY, PLANES)
    def _(j):
        for side in range(2):
            halo(j, xs, side).start()

    @pl.loop(0, PLANES + LAG2)
    def _(i):
        @pl.when(i < PLANES)
        def _():
            step_x(i)

        @pl.when((i >= LAGZ) & (i < LAGZ + PLANES))
        def _():
            step_z(i - LAGZ)

        @pl.when((i >= LAGY) & (i < LAGY + PLANES - EARLY))
        def _():
            step_y(i + EARLY - LAGY)

        @pl.when((i >= LAG1) & (i < LAG1 + EARLY))
        def _():
            early_halo(i - LAG1)

        @pl.when((i >= LAG2) & (i < LAG2 + EARLY))
        def _():
            early_finish(i - LAG2)

        @pl.when(i >= LAG2 + EARLY)
        def _():
            late_finish(i - LAG2)

    for k in hops:
        home(PLANES - 1, k).wait_send()


def write_out(detail, coarse, detail_ref, coarse_ref, sem):
    copies = [pltpu.make_async_copy(src.at[j], dst.at[j], sem.at[i, j])
              for j in range(PLANES) for i, (src, dst) in enumerate(((detail, detail_ref), (coarse, coarse_ref)))]
    for copy in copies:
        copy.start()
    for copy in copies:
        copy.wait()


def shards(coarse_six):
    full = pltpu.VMEM((PLANES, ROWS, COLS), F32)

    def packed(n):
        return pltpu.VMEM((PLANES, n, 8 * SENT, 128), F32)

    edge = pltpu.VMEM((PLANES, HALO, COLS), F32)
    dma = pltpu.SemaphoreType.DMA
    n = len(HOPS)
    results = pl.pallas_call(
        kernel,
        out_shape=(full, full),
        in_specs=[pl.BlockSpec(memory_space=pl.ANY)],
        out_specs=(pl.BlockSpec(memory_space=pltpu.VMEM),) * 2,
        scratch_shapes=[full, full, packed(RING), pltpu.VMEM((ROWS, 128), F32), packed(RING + 4), packed(RING), packed(RING),
                        pltpu.VMEM((EARLY, ROWS, COLS), F32), edge, edge,
                        pltpu.SemaphoreType.REGULAR, pltpu.SemaphoreType.REGULAR, dma((PLANES,)), dma((RING,)), dma((PLANES, n)), dma((PLANES, n)), dma((PLANES, n)), dma((PLANES, n)),
                        dma((PLANES, 2)), dma((PLANES, 2)), dma((PLANES, 2)), dma((PLANES, 2))],
        compiler_params=pltpu.CompilerParams(collective_id=0, has_side_effects=True, vmem_limit_bytes=50 << 20),
        name="starlet",
    )(coarse_six)
    block = jax.ShapeDtypeStruct((PLANES, ROWS, COLS), F32)
    return pl.pallas_call(
        write_out,
        out_shape=(block, block),
        in_specs=[pl.BlockSpec(memory_space=pl.ANY)] * 2,
        out_specs=(pl.BlockSpec(memory_space=pl.ANY),) * 2,
        scratch_shapes=[dma((2, PLANES))],
        compiler_params=pltpu.CompilerParams(vmem_limit_bytes=1 << 20),
        name="write_out",
    )(*results)


def solution(mesh):
    return jax.shard_map(
        shards,
        mesh=mesh,
        in_specs=(P("gz", "gy", None),),
        out_specs=(P("gz", "gy", None), P("gz", "gy", None)),
        check_vma=False,
    )
```

```python
import functools

import jax
import jax.numpy as jnp
from jax import lax
from jax.experimental import pallas as pl
from jax.experimental.pallas import tpu as pltpu
from jax.sharding import PartitionSpec as P

MESH = pl.DeviceIdType.MESH
F32 = jnp.float32

PLANES, ROWS, COLS = 8, 256, 512
RING = 4
PIECE = ROWS // RING
TILES = PIECE // 8
SENT = 3 * TILES + TILES - 2
DIL = 32
HALO = 2 * DIL
EARLY = 5
LAGY, LAGZ, LAG1, LAG2 = 1, 1, 4, 6
SCALE = 1.0 / 4096.0
HOPS = (1, 3, 2)


def place():
    g, h = lax.axis_index("gz"), lax.axis_index("gy")
    return g // 16, (g // 4) % 4, g % 4, h


def device(dx, dy):
    x, y, r, h = place()
    return (((x + dx) % 4) * 16 + ((y + dy) % 4) * 4 + r, h)


def ring_index(dy):
    return (place()[1] + dy) % 4


def gy_device(dh):
    g, h = lax.axis_index("gz"), lax.axis_index("gy")
    return (g, (h + dh) % 4)


def tile(start):
    return pl.ds(pl.multiple_of(start, 8), 8)


def smooth_x(src, j, emit, first=0, count=ROWS // 32):
    lane = lax.broadcasted_iota(jnp.int32, (8, 128), 1)
    left, low, high = lane < 64, lane < 96, lane >= 32

    @pl.loop(first, first + count)
    def _(t):
        for u in range(4):
            v = [src[j, tile(t * 32 + 8 * u), 128 * k : 128 * k + 128] for k in range(4)]
            up = [pltpu.roll(a, 96, 1) for a in v]
            half = [pltpu.roll(a, 64, 1) for a in v]
            down = [pltpu.roll(a, 32, 1) for a in v]
            for k in range(4):
                after, before = (k + 1) % 4, (k + 3) % 4
                near = jnp.where(low, up[k], up[after]) + jnp.where(high, down[k], down[before])
                far = half[k] + jnp.where(left, half[before], half[after])
                emit(t, 8 * u, k, 6.0 * v[k] + (4.0 * near + far))


def smooth_y(src, before, after, j, emit):
    @pl.loop(0, DIL // 8)
    def _(t):
        for k in range(4):
            cols = slice(128 * k, 128 * k + 128)

            def at(ref, start):
                return ref[j, tile(start + t * 8), cols]

            v = [at(before, 0), at(before, DIL)]
            v += [at(src, DIL * i) for i in range(ROWS // DIL)]
            v += [at(after, 0), at(after, DIL)]
            for _ in range(4):
                v = [v[i] + v[i + 1] for i in range(len(v) - 1)]
            for i in range(ROWS // DIL):
                emit(i, t * 8, k, v[i])


def pack_last(column, dst, j, p):
    low = lax.broadcasted_iota(jnp.int32, (8, 128), 1) < 96
    v = [column[tile(PIECE * p + 8 * t), :] for t in range(TILES)]
    for t in range(TILES - 2):
        moved = pltpu.roll(v[TILES - 2 + t // 3], 96 - 32 * (t % 3), 1)
        dst[j, p, 8 * (3 * TILES + t) : 8 * (3 * TILES + t) + 8, :] = jnp.where(low, v[t], moved)


def unpack(src, j, p, emit):
    lane = lax.broadcasted_iota(jnp.int32, (8, 128), 1)
    low, one, two = lane < 96, lane < 32, lane < 64
    odd = (lane // 32) % 2 == 1

    last = [src[j, p, 8 * (3 * TILES + t) : 8 * (3 * TILES + t) + 8, :] for t in range(TILES - 2)]
    for t in (0, 3):
        r = [pltpu.roll(last[t + i], 32 * i + 32, 1) for i in range(3)]
        last.append(jnp.where(one, r[0], jnp.where(two, r[1], r[2])))
    for t in range(TILES):
        v = [src[j, p, 8 * (k * TILES + t) : 8 * (k * TILES + t) + 8, :] for k in range(3)]
        total = (v[0] + v[1]) + (v[2] + jnp.where(low, last[t], 0.0))
        total = jnp.where(odd, -total, total)
        total = total + pltpu.roll(total, 64, 1)
        total = total + pltpu.roll(total, 32, 1)
        v.append(jnp.where(low, last[t], total))
        for k in range(4):
            emit(p, 8 * t, k, v[k])


def smooth_z(src, dst, j):
    @pl.loop(0, SENT // 3)
    def _(t):
        for u in range(3):
            rows = tile(t * 24 + 8 * u)
            v = [src[j, q, rows, :] for q in range(RING + 4)]
            for _ in range(4):
                v = [v[q] + v[q + 1] for q in range(len(v) - 1)]
            for q in range(RING):
                dst[j, q, rows, :] = v[q] * SCALE


def kernel(x_ref, detail, coarse, xin, back, xs, ys, column, gathered, smoothed, early, before, after,
           ring_sem, near_sem, load_sem, first_sem, f_send, f_recv, b_send, b_recv, h_send, h_recv, x_send, x_recv):
    me = ring_index(0)
    hops = range(len(HOPS))

    def load(j):
        return pltpu.make_async_copy(x_ref.at[j], xin.at[j], load_sem.at[j])

    def load_first(dy):
        rows = pl.ds(pl.multiple_of(PIECE * ring_index(dy), PIECE), PIECE)
        return pltpu.make_async_copy(x_ref.at[0, rows], xin.at[0, rows], first_sem.at[dy])

    def forth(j, k):
        dy = HOPS[k]
        return pltpu.make_async_remote_copy(
            ys.at[j, ring_index(dy)], gathered.at[j, me + 2], f_send.at[j, k], f_recv.at[j, k],
            device_id=device(0, dy), device_id_type=MESH)

    def home(j, k):
        dy = HOPS[k]
        return pltpu.make_async_remote_copy(
            smoothed.at[j, ring_index(dy)], back.at[j, me], b_send.at[j, k], b_recv.at[j, k],
            device_id=device(0, dy), device_id_type=MESH)

    def halo(j, src, side):
        if side == 0:
            return pltpu.make_async_remote_copy(
                src.at[j, pl.ds(ROWS - HALO, HALO)], before.at[j], h_send.at[j, 0], h_recv.at[j, 0],
                device_id=gy_device(1), device_id_type=MESH)
        return pltpu.make_async_remote_copy(
            src.at[j, pl.ds(0, HALO)], after.at[j], h_send.at[j, 1], h_recv.at[j, 1],
            device_id=gy_device(3), device_id_type=MESH)

    def emit_packed(j, block, row, k, value):
        if k < 3:
            ys[j, block // 2, tile(PIECE * k + 32 * (block % 2) + row), :] = value
        else:
            column[tile(32 * block + row), :] = value

    def send_forth(j):
        for k in hops:
            pack_last(column, ys, j, ring_index(HOPS[k]))
            forth(j, k).start()
        pack_last(column, ys, j, me)
        gathered[j, me + 2] = ys[j, me]

    def across(j, side):
        src, dst, dx = ((4, 0, 1), (2, 6, 3))[side]
        return pltpu.make_async_remote_copy(
            gathered.at[j, pl.ds(src, 2)], gathered.at[j, pl.ds(dst, 2)], x_send.at[j, side], x_recv.at[j, side],
            device_id=device(dx, 0), device_id_type=MESH)

    def step_x(j):
        for k in hops:
            forth(j, k).wait_recv()
        for side in range(2):
            across(j, side).start()

    def step_z(j):
        for side in range(2):
            across(j, side).wait_recv()
        smooth_z(gathered, smoothed, j)
        for k in hops:
            home(j, k).start()
        back[j, me] = smoothed[j, me]

    def step_y(j):
        for side in range(2):
            halo(j, xs, side).wait_recv()
        smooth_y(xs, before, after, j, lambda block, row, k, value: emit_packed(j, block, row, k, value))
        send_forth(j)

    def arrive(j, emit):
        unpack(back, j, me, emit)
        for k in hops:
            home(j, k).wait_recv()
            unpack(back, j, ring_index(-HOPS[k]), emit)

    def early_halo(j):
        def emit(p, row, k, value):
            early[j, tile(PIECE * p + row), 128 * k : 128 * k + 128] = value

        arrive(j, emit)
        for side in range(2):
            halo(j, early, side).start()

    def emit_out(j, start, k, value):
        rows, cols = tile(start), slice(128 * k, 128 * k + 128)
        coarse[j, rows, cols] = value
        detail[j, rows, cols] = xin[j, rows, cols] - value

    def early_finish(j):
        for side in range(2):
            halo(j, early, side).wait_recv()
        sent(j)
        smooth_y(early, before, after, j, lambda block, row, k, value: emit_out(j, 32 * block + row, k, value))

    def sent(j):
        for side in range(2):
            halo(j, xs, side).wait_send()
            across(j, side).wait_send()
        for k in hops:
            forth(j, k).wait_send()

        @pl.when(j > 0)
        def _():
            for k in hops:
                home(j - 1, k).wait_send()

    def late_finish(j):
        sent(j)

        @pl.when(j < PLANES - 1)
        def _():
            arrive(j, lambda p, row, k, value: emit_out(j, PIECE * p + row, k, value))

        @pl.when(j == PLANES - 1)
        def _():
            for k in hops:
                home(j, k).wait_recv()

    def early_start(j):
        smooth_x(xin, j, lambda block, row, k, value: emit_packed(j, block, row, k, value))

    def late_start(j):
        def emit(block, row, k, value):
            xs[j, tile(32 * block + row), 128 * k : 128 * k + 128] = value

        smooth_x(xin, j, emit)

    for dy in HOPS + (0,):
        load_first(dy).start()
    y = place()[1]
    barrier = pltpu.get_barrier_semaphore()
    for dy in HOPS:
        @pl.when((y + dy) % 4 != 0)
        def _():
            pl.semaphore_signal(barrier, inc=1, device_id=device(0, dy), device_id_type=MESH)

    for j in range(1, PLANES):
        load(j).start()

    def first_piece(dy):
        load_first(dy).wait()
        p = ring_index(dy)
        smooth_x(xin, 0, lambda block, row, k, value: emit_packed(0, block, row, k, value), 2 * p, 2)
        pack_last(column, ys, 0, p)

    first_piece(HOPS[0])

    @pl.when(y != 0)
    def _():
        pl.semaphore_wait(barrier, 3)
        pl.semaphore_signal(ring_sem, inc=1, device_id=device(0, 4 - y), device_id_type=MESH)

    @pl.when(y == 0)
    def _():
        pl.semaphore_wait(ring_sem, 3)
        for there in (device(1, 0), device(3, 0), gy_device(1), gy_device(3)):
            pl.semaphore_signal(barrier, inc=1, device_id=there, device_id_type=MESH)

    forth(0, 0).start()
    for k in hops[1:]:
        first_piece(HOPS[k])
        forth(0, k).start()
    first_piece(0)
    gathered[0, me + 2] = ys[0, me]

    @pl.loop(1, EARLY)
    def _(j):
        load(j).wait()
        early_start(j)
        send_forth(j)

    @pl.loop(EARLY, PLANES)
    def _(j):
        load(j).wait()
        late_start(j)

    @pl.when(y == 0)
    def _():
        pl.semaphore_wait(barrier, 4)
        for dy in HOPS:
            pl.semaphore_signal(near_sem, inc=1, device_id=device(0, dy), device_id_type=MESH)

    @pl.when(y != 0)
    def _():
        pl.semaphore_wait(near_sem, 1)

    @pl.loop(EARLY, PLANES)
    def _(j):
        for side in range(2):
            halo(j, xs, side).start()

    @pl.loop(0, PLANES + LAG2)
    def _(i):
        @pl.when(i < PLANES)
        def _():
            step_x(i)

        @pl.when((i >= LAGZ) & (i < LAGZ + PLANES))
        def _():
            step_z(i - LAGZ)

        @pl.when((i >= LAGY) & (i < LAGY + PLANES - EARLY))
        def _():
            step_y(i + EARLY - LAGY)

        @pl.when((i >= LAG1) & (i < LAG1 + EARLY))
        def _():
            early_halo(i - LAG1)

        @pl.when((i >= LAG2) & (i < LAG2 + EARLY))
        def _():
            early_finish(i - LAG2)

        @pl.when(i >= LAG2 + EARLY)
        def _():
            late_finish(i - LAG2)

    for k in hops:
        home(PLANES - 1, k).wait_send()


def write_out(detail, coarse, xin, back, detail_ref, coarse_ref, last_detail, last_coarse, sem):
    last = PLANES - 1
    copies = [pltpu.make_async_copy(src.at[j], dst.at[j], sem.at[i, j])
              for j in range(last) for i, (src, dst) in enumerate(((detail, detail_ref), (coarse, coarse_ref)))]
    for copy in copies:
        copy.start()

    def emit(p, row, k, value):
        rows, cols = tile(PIECE * p + row), slice(128 * k, 128 * k + 128)
        last_coarse[rows, cols] = value
        last_detail[rows, cols] = xin[last, rows, cols] - value

    @pl.loop(0, RING)
    def _(p):
        unpack(back, last, p, emit)

    ends = [pltpu.make_async_copy(src, dst.at[last], sem.at[i, last])
            for i, (src, dst) in enumerate(((last_detail, detail_ref), (last_coarse, coarse_ref)))]
    for copy in ends:
        copy.start()
    for copy in copies + ends:
        copy.wait()


def shards(coarse_six):
    full = pltpu.VMEM((PLANES, ROWS, COLS), F32)

    def packed(n):
        return pltpu.VMEM((PLANES, n, 8 * SENT, 128), F32)

    edge = pltpu.VMEM((PLANES, HALO, COLS), F32)
    dma = pltpu.SemaphoreType.DMA
    n = len(HOPS)
    results = pl.pallas_call(
        kernel,
        out_shape=(full, full, full, packed(RING)),
        in_specs=[pl.BlockSpec(memory_space=pl.ANY)],
        out_specs=(pl.BlockSpec(memory_space=pltpu.VMEM),) * 4,
        scratch_shapes=[full, packed(RING), pltpu.VMEM((ROWS, 128), F32), packed(RING + 4), packed(RING),
                        pltpu.VMEM((EARLY, ROWS, COLS), F32), edge, edge,
                        pltpu.SemaphoreType.REGULAR, pltpu.SemaphoreType.REGULAR, dma((PLANES,)), dma((RING,)), dma((PLANES, n)), dma((PLANES, n)), dma((PLANES, n)), dma((PLANES, n)),
                        dma((PLANES, 2)), dma((PLANES, 2)), dma((PLANES, 2)), dma((PLANES, 2))],
        compiler_params=pltpu.CompilerParams(collective_id=0, has_side_effects=True, vmem_limit_bytes=42 << 20),
        name="starlet",
    )(coarse_six)
    block = jax.ShapeDtypeStruct((PLANES, ROWS, COLS), F32)
    return pl.pallas_call(
        write_out,
        out_shape=(block, block),
        in_specs=[pl.BlockSpec(memory_space=pl.ANY)] * 2 + [pl.BlockSpec(memory_space=pltpu.VMEM)] * 2,
        out_specs=(pl.BlockSpec(memory_space=pl.ANY),) * 2,
        scratch_shapes=[pltpu.VMEM((ROWS, COLS), F32), pltpu.VMEM((ROWS, COLS), F32), dma((2, PLANES))],
        compiler_params=pltpu.CompilerParams(vmem_limit_bytes=16 << 20),
        name="write_out",
    )(*results)


def solution(mesh):
    return jax.shard_map(
        shards,
        mesh=mesh,
        in_specs=(P("gz", "gy", None),),
        out_specs=(P("gz", "gy", None), P("gz", "gy", None)),
        check_vma=False,
    )
```

```python
import functools

import jax
import jax.numpy as jnp
from jax import lax
from jax.experimental import pallas as pl
from jax.experimental.pallas import tpu as pltpu
from jax.sharding import PartitionSpec as P

MESH = pl.DeviceIdType.MESH
F32 = jnp.float32

PLANES, ROWS, COLS = 8, 256, 512
RING = 4
PIECE = ROWS // RING
TILES = PIECE // 8
SENT = 3 * TILES + TILES - 2
DIL = 32
HALO = 2 * DIL
EARLY = 5
LAGY, LAGZ, LAG1, LAG2 = 1, 1, 3, 5
SCALE = 1.0 / 4096.0
HOPS = (1, 3, 2)


def place():
    g, h = lax.axis_index("gz"), lax.axis_index("gy")
    return g // 16, (g // 4) % 4, g % 4, h


def device(dx, dy):
    x, y, r, h = place()
    return (((x + dx) % 4) * 16 + ((y + dy) % 4) * 4 + r, h)


def ring_index(dy):
    return (place()[1] + dy) % 4


def gy_device(dh):
    g, h = lax.axis_index("gz"), lax.axis_index("gy")
    return (g, (h + dh) % 4)


def tile(start):
    return pl.ds(pl.multiple_of(start, 8), 8)


def smooth_x(src, j, emit, first=0, count=ROWS // 32):
    lane = lax.broadcasted_iota(jnp.int32, (8, 128), 1)
    left, low, high = lane < 64, lane < 96, lane >= 32

    @pl.loop(first, first + count)
    def _(t):
        for u in range(4):
            v = [src[j, tile(t * 32 + 8 * u), 128 * k : 128 * k + 128] for k in range(4)]
            up = [pltpu.roll(a, 96, 1) for a in v]
            half = [pltpu.roll(a, 64, 1) for a in v]
            down = [pltpu.roll(a, 32, 1) for a in v]
            for k in range(4):
                after, before = (k + 1) % 4, (k + 3) % 4
                near = jnp.where(low, up[k], up[after]) + jnp.where(high, down[k], down[before])
                far = half[k] + jnp.where(left, half[before], half[after])
                emit(t, 8 * u, k, 6.0 * v[k] + (4.0 * near + far))


def smooth_y(src, before, after, j, emit):
    @pl.loop(0, DIL // 8)
    def _(t):
        for k in range(4):
            cols = slice(128 * k, 128 * k + 128)

            def at(ref, start):
                return ref[j, tile(start + t * 8), cols]

            v = [at(before, 0), at(before, DIL)]
            v += [at(src, DIL * i) for i in range(ROWS // DIL)]
            v += [at(after, 0), at(after, DIL)]
            for _ in range(4):
                v = [v[i] + v[i + 1] for i in range(len(v) - 1)]
            for i in range(ROWS // DIL):
                emit(i, t * 8, k, v[i])


def pack_last(column, dst, j, p):
    low = lax.broadcasted_iota(jnp.int32, (8, 128), 1) < 96
    v = [column[tile(PIECE * p + 8 * t), :] for t in range(TILES)]
    for t in range(TILES - 2):
        moved = pltpu.roll(v[TILES - 2 + t // 3], 96 - 32 * (t % 3), 1)
        dst[j, p, 8 * (3 * TILES + t) : 8 * (3 * TILES + t) + 8, :] = jnp.where(low, v[t], moved)


def unpack(src, j, p, emit):
    lane = lax.broadcasted_iota(jnp.int32, (8, 128), 1)
    low, one, two = lane < 96, lane < 32, lane < 64
    odd = (lane // 32) % 2 == 1

    last = [src[j, p, 8 * (3 * TILES + t) : 8 * (3 * TILES + t) + 8, :] for t in range(TILES - 2)]
    for t in (0, 3):
        r = [pltpu.roll(last[t + i], 32 * i + 32, 1) for i in range(3)]
        last.append(jnp.where(one, r[0], jnp.where(two, r[1], r[2])))
    for t in range(TILES):
        v = [src[j, p, 8 * (k * TILES + t) : 8 * (k * TILES + t) + 8, :] for k in range(3)]
        total = (v[0] + v[1]) + (v[2] + jnp.where(low, last[t], 0.0))
        total = jnp.where(odd, -total, total)
        total = total + pltpu.roll(total, 64, 1)
        total = total + pltpu.roll(total, 32, 1)
        v.append(jnp.where(low, last[t], total))
        for k in range(4):
            emit(p, 8 * t, k, v[k])


def smooth_z(src, dst, j):
    @pl.loop(0, SENT // 3)
    def _(t):
        for u in range(3):
            rows = tile(t * 24 + 8 * u)
            v = [src[j, q, rows, :] for q in range(RING + 4)]
            for _ in range(4):
                v = [v[q] + v[q + 1] for q in range(len(v) - 1)]
            for q in range(RING):
                dst[j, q, rows, :] = v[q] * SCALE


def kernel(x_ref, detail, coarse, xin, back, xs, ys, column, gathered, smoothed, early, before, after,
           ring_sem, near_sem, load_sem, first_sem, f_send, f_recv, b_send, b_recv, h_send, h_recv, x_send, x_recv):
    me = ring_index(0)
    hops = range(len(HOPS))

    def load(j):
        return pltpu.make_async_copy(x_ref.at[j], xin.at[j], load_sem.at[j])

    def load_first(dy):
        rows = pl.ds(pl.multiple_of(PIECE * ring_index(dy), PIECE), PIECE)
        return pltpu.make_async_copy(x_ref.at[0, rows], xin.at[0, rows], first_sem.at[dy])

    def forth(j, k):
        dy = HOPS[k]
        return pltpu.make_async_remote_copy(
            ys.at[j, ring_index(dy)], gathered.at[j, me + 2], f_send.at[j, k], f_recv.at[j, k],
            device_id=device(0, dy), device_id_type=MESH)

    def home(j, k):
        dy = HOPS[k]
        return pltpu.make_async_remote_copy(
            smoothed.at[j, ring_index(dy)], back.at[j, me], b_send.at[j, k], b_recv.at[j, k],
            device_id=device(0, dy), device_id_type=MESH)

    def halo(j, src, side):
        if side == 0:
            return pltpu.make_async_remote_copy(
                src.at[j, pl.ds(ROWS - HALO, HALO)], before.at[j], h_send.at[j, 0], h_recv.at[j, 0],
                device_id=gy_device(1), device_id_type=MESH)
        return pltpu.make_async_remote_copy(
            src.at[j, pl.ds(0, HALO)], after.at[j], h_send.at[j, 1], h_recv.at[j, 1],
            device_id=gy_device(3), device_id_type=MESH)

    def emit_packed(j, block, row, k, value):
        if k < 3:
            ys[j, block // 2, tile(PIECE * k + 32 * (block % 2) + row), :] = value
        else:
            column[tile(32 * block + row), :] = value

    def send_forth(j):
        for k in hops:
            pack_last(column, ys, j, ring_index(HOPS[k]))
            forth(j, k).start()
        pack_last(column, ys, j, me)
        gathered[j, me + 2] = ys[j, me]

    def across(j, side):
        src, dst, dx = ((4, 0, 1), (2, 6, 3))[side]
        return pltpu.make_async_remote_copy(
            gathered.at[j, pl.ds(src, 2)], gathered.at[j, pl.ds(dst, 2)], x_send.at[j, side], x_recv.at[j, side],
            device_id=device(dx, 0), device_id_type=MESH)

    def step_x(j):
        for k in hops:
            forth(j, k).wait_recv()
        for side in range(2):
            across(j, side).start()

    def step_z(j):
        for side in range(2):
            across(j, side).wait_recv()
        smooth_z(gathered, smoothed, j)
        for k in hops:
            home(j, k).start()
        back[j, me] = smoothed[j, me]

    def step_y(j):
        for side in range(2):
            halo(j, xs, side).wait_recv()
        smooth_y(xs, before, after, j, lambda block, row, k, value: emit_packed(j, block, row, k, value))
        send_forth(j)

    def arrive(j, emit):
        unpack(back, j, me, emit)
        for k in hops:
            home(j, k).wait_recv()
            unpack(back, j, ring_index(-HOPS[k]), emit)

    def early_halo(j):
        def emit(p, row, k, value):
            early[j, tile(PIECE * p + row), 128 * k : 128 * k + 128] = value

        arrive(j, emit)
        for side in range(2):
            halo(j, early, side).start()

    def emit_out(j, start, k, value):
        rows, cols = tile(start), slice(128 * k, 128 * k + 128)
        coarse[j, rows, cols] = value
        detail[j, rows, cols] = xin[j, rows, cols] - value

    def early_finish(j):
        for side in range(2):
            halo(j, early, side).wait_recv()
        sent(j)
        smooth_y(early, before, after, j, lambda block, row, k, value: emit_out(j, 32 * block + row, k, value))

    def sent(j):
        for side in range(2):
            halo(j, xs, side).wait_send()
            across(j, side).wait_send()
        for k in hops:
            forth(j, k).wait_send()

        @pl.when(j > 0)
        def _():
            for k in hops:
                home(j - 1, k).wait_send()

    def late_finish(j):
        sent(j)

        @pl.when(j < PLANES - 1)
        def _():
            arrive(j, lambda p, row, k, value: emit_out(j, PIECE * p + row, k, value))

        @pl.when(j == PLANES - 1)
        def _():
            for k in hops:
                home(j, k).wait_recv()

    def early_start(j):
        smooth_x(xin, j, lambda block, row, k, value: emit_packed(j, block, row, k, value))

    def late_start(j):
        def emit(block, row, k, value):
            xs[j, tile(32 * block + row), 128 * k : 128 * k + 128] = value

        smooth_x(xin, j, emit)

    for dy in HOPS + (0,):
        load_first(dy).start()
    y = place()[1]
    barrier = pltpu.get_barrier_semaphore()
    for dy in HOPS:
        @pl.when((y + dy) % 4 != 0)
        def _():
            pl.semaphore_signal(barrier, inc=1, device_id=device(0, dy), device_id_type=MESH)

    for j in range(1, PLANES):
        load(j).start()

    def first_piece(dy):
        load_first(dy).wait()
        p = ring_index(dy)
        smooth_x(xin, 0, lambda block, row, k, value: emit_packed(0, block, row, k, value), 2 * p, 2)
        pack_last(column, ys, 0, p)

    first_piece(HOPS[0])

    @pl.when(y != 0)
    def _():
        pl.semaphore_wait(barrier, 3)
        pl.semaphore_signal(ring_sem, inc=1, device_id=device(0, 4 - y), device_id_type=MESH)

    @pl.when(y == 0)
    def _():
        pl.semaphore_wait(ring_sem, 3)
        for there in (device(1, 0), device(3, 0), gy_device(1), gy_device(3)):
            pl.semaphore_signal(barrier, inc=1, device_id=there, device_id_type=MESH)

    forth(0, 0).start()
    for k in hops[1:]:
        first_piece(HOPS[k])
        forth(0, k).start()
    first_piece(0)
    gathered[0, me + 2] = ys[0, me]

    @pl.loop(1, EARLY)
    def _(j):
        load(j).wait()
        early_start(j)
        send_forth(j)

    @pl.loop(EARLY, PLANES)
    def _(j):
        load(j).wait()
        late_start(j)

    @pl.when(y == 0)
    def _():
        pl.semaphore_wait(barrier, 4)
        for dy in HOPS:
            pl.semaphore_signal(near_sem, inc=1, device_id=device(0, dy), device_id_type=MESH)

    @pl.when(y != 0)
    def _():
        pl.semaphore_wait(near_sem, 1)

    @pl.loop(EARLY, PLANES)
    def _(j):
        for side in range(2):
            halo(j, xs, side).start()

    @pl.loop(0, PLANES + LAG2)
    def _(i):
        @pl.when(i < PLANES)
        def _():
            step_x(i)

        @pl.when((i >= LAGZ) & (i < LAGZ + PLANES))
        def _():
            step_z(i - LAGZ)

        @pl.when((i >= LAGY) & (i < LAGY + PLANES - EARLY))
        def _():
            step_y(i + EARLY - LAGY)

        @pl.when((i >= LAG1) & (i < LAG1 + EARLY))
        def _():
            early_halo(i - LAG1)

        @pl.when((i >= LAG2) & (i < LAG2 + EARLY))
        def _():
            early_finish(i - LAG2)

        @pl.when(i >= LAG2 + EARLY)
        def _():
            late_finish(i - LAG2)

    for k in hops:
        home(PLANES - 1, k).wait_send()


def write_out(detail, coarse, xin, back, detail_ref, coarse_ref, last_detail, last_coarse, sem):
    last = PLANES - 1
    copies = [pltpu.make_async_copy(src.at[j], dst.at[j], sem.at[i, j])
              for j in range(last) for i, (src, dst) in enumerate(((detail, detail_ref), (coarse, coarse_ref)))]
    for copy in copies:
        copy.start()

    def emit(p, row, k, value):
        rows, cols = tile(PIECE * p + row), slice(128 * k, 128 * k + 128)
        last_coarse[rows, cols] = value
        last_detail[rows, cols] = xin[last, rows, cols] - value

    @pl.loop(0, RING)
    def _(p):
        unpack(back, last, p, emit)

    ends = [pltpu.make_async_copy(src, dst.at[last], sem.at[i, last])
            for i, (src, dst) in enumerate(((last_detail, detail_ref), (last_coarse, coarse_ref)))]
    for copy in ends:
        copy.start()
    for copy in copies + ends:
        copy.wait()


def shards(coarse_six):
    full = pltpu.VMEM((PLANES, ROWS, COLS), F32)

    def packed(n):
        return pltpu.VMEM((PLANES, n, 8 * SENT, 128), F32)

    edge = pltpu.VMEM((PLANES, HALO, COLS), F32)
    dma = pltpu.SemaphoreType.DMA
    n = len(HOPS)
    results = pl.pallas_call(
        kernel,
        out_shape=(full, full, full, packed(RING)),
        in_specs=[pl.BlockSpec(memory_space=pl.ANY)],
        out_specs=(pl.BlockSpec(memory_space=pltpu.VMEM),) * 4,
        scratch_shapes=[full, packed(RING), pltpu.VMEM((ROWS, 128), F32), packed(RING + 4), packed(RING),
                        pltpu.VMEM((EARLY, ROWS, COLS), F32), edge, edge,
                        pltpu.SemaphoreType.REGULAR, pltpu.SemaphoreType.REGULAR, dma((PLANES,)), dma((RING,)), dma((PLANES, n)), dma((PLANES, n)), dma((PLANES, n)), dma((PLANES, n)),
                        dma((PLANES, 2)), dma((PLANES, 2)), dma((PLANES, 2)), dma((PLANES, 2))],
        compiler_params=pltpu.CompilerParams(collective_id=0, has_side_effects=True, vmem_limit_bytes=42 << 20),
        name="starlet",
    )(coarse_six)
    block = jax.ShapeDtypeStruct((PLANES, ROWS, COLS), F32)
    return pl.pallas_call(
        write_out,
        out_shape=(block, block),
        in_specs=[pl.BlockSpec(memory_space=pl.ANY)] * 2 + [pl.BlockSpec(memory_space=pltpu.VMEM)] * 2,
        out_specs=(pl.BlockSpec(memory_space=pl.ANY),) * 2,
        scratch_shapes=[pltpu.VMEM((ROWS, COLS), F32), pltpu.VMEM((ROWS, COLS), F32), dma((2, PLANES))],
        compiler_params=pltpu.CompilerParams(vmem_limit_bytes=16 << 20),
        name="write_out",
    )(*results)


def solution(mesh):
    return jax.shard_map(
        shards,
        mesh=mesh,
        in_specs=(P("gz", "gy", None),),
        out_specs=(P("gz", "gy", None), P("gz", "gy", None)),
        check_vma=False,
    )
```
